256 devices in a mesh: slab: 32 (over z, x_lo, core), blk: 8 (over x_hi, y).
Axes of the slice: x: 4 (x_hi: 2, x_lo: 2; x = x_hi * 2 + x_lo), y: 4, z: 8, core: 2. Of those that a mesh axis runs over, the one named last changes fastest.
Arguments:
- modes: bfloat16 [131072, 2048], P('slab', 'blk'), may hold values from -6 to 6
- stiffness: bfloat16 [131072, 512], P('slab'), may hold values from -0.0007324219 to 0.0007324219
- offsets: int32 [2048, 8], P('slab'), may hold values from -4 to 4, as said below
Outputs:
- reduced: float32 [2048, 2048], P('blk', 'slab')
The draws below stay inside these ranges and needn't reach their ends.
Inputs may be any that keep to these rules, and one draw needn't show every extreme that they name: Each row of offsets lists 8 different values, in an order drawn from the seed: all of -4 to 4 except one nonzero value of magnitude below 4.
All inputs are finite; a program needn't handle non-finite values.
Results may differ from the reference program's by a relative error of at most 0.0029.
Values may be sent and summed in bfloat16 or wider, within the bound.
A program may use at most 128 MiB of HBM per device.

```python
import jax
import jax.numpy as jnp
from jax import lax

M = 2048
BS = 64
HB = 4
BPR = 8
NDOF = 131072
NBR = 2048


def draw_offsets(key, part):
    row_keys = jax.random.split(key, NBR)
    magnitude = jax.random.randint(jax.random.fold_in(key, 7), (NBR,), 1, HB)
    signs = jax.random.randint(jax.random.fold_in(key, 11), (NBR,), 0, 2) * 2 - 1
    dropped = magnitude * signs
    slots = jnp.arange(BPR, dtype=jnp.int32)
    values = -HB + slots[None, :] + (slots[None, :] >= (dropped + HB)[:, None]).astype(jnp.int32)
    orders = jax.vmap(lambda k: jax.random.permutation(k, BPR))(row_keys)
    return jnp.take_along_axis(values, orders, axis=1).astype(jnp.int32)


def with_spikes(array, stream_key, source, target, blocks, factor):
    def block_of(axis_at):
        return (jnp.arange(array.shape[axis_at]) // (array.shape[axis_at] // blocks)).reshape((-1,) + (1,) * (array.ndim - 1 - axis_at))

    one_side = jax.random.permutation(stream_key, blocks)[block_of(target)]
    far = (block_of(target) + blocks // 2) % blocks
    return jnp.where((block_of(source) == one_side) | (block_of(source) == far), factor * array, array)


def block_levels(own_key, extent, shards, least, top_value):
    gain = 1.0
    for dim, blocks in shards:
        steps = jax.random.uniform(jax.random.fold_in(jax.random.fold_in(own_key, 6), dim), (blocks,), jnp.float32, least / len(shards), top_value / len(shards))
        gain = gain * jnp.repeat(jnp.exp(steps), extent[dim] // blocks).reshape((-1,) + (1,) * (len(extent) - 1 - dim))
    return gain


def centred(rng, shape, deviation, reach, cuts=(), kind=jnp.bfloat16):
    entries = jax.random.normal(rng, shape, jnp.float32) * deviation
    if len(cuts) > 0:
        entries = block_levels(rng, shape, cuts, -0.22, 0.18) * entries
    return jnp.clip(entries, min=-reach, max=reach).astype(kind)


def heavy_noise(stream_key, dims, scale, reach, shards, heavy, kind=jnp.bfloat16):
    result = scale * jax.random.normal(stream_key, dims, jnp.float32)
    if shards:
        result = result * block_levels(stream_key, dims, shards, -0.22, 0.18)
    return jnp.clip(with_spikes(result, jax.random.fold_in(stream_key, 3), *heavy), -reach, reach).astype(kind)


def setup_inputs(seed: int = 0) -> dict:
    splits = jax.random.split(jax.random.key(seed), 4)
    return {
        "modes": heavy_noise(splits[0], (NDOF, M), 1.0, 6.0, ((0, 32), (1, 8)), (0, 1, 32, 2.75)),
        "stiffness": centred(splits[1], (NDOF, BPR * BS), (BPR * BS * NDOF) ** -0.5, 0.0007324219, ((0, 32),)),
        "offsets": draw_offsets(jax.random.fold_in(splits[3], 71), 0),
    }


def reference(modes, stiffness, offsets):
    rim = HB * BS
    padded = jnp.pad(modes.astype(jnp.float32), ((rim, rim), (0, 0)))
    blocks = padded.reshape(NBR + 2 * HB, BS, M)
    kblocks = stiffness.astype(jnp.float32).reshape(NBR, BS, BPR, BS)
    base = jnp.arange(NBR, dtype=jnp.int32)
    total = jnp.zeros((NBR, BS, M), jnp.float32)
    for column in range(BPR):
        where = (base + offsets[:, column] + HB).astype(jnp.int32)
        picked = jnp.take(blocks, where, axis=0)
        total = total + jnp.einsum("nab,nbm->nam", kblocks[:, :, column, :], picked, precision=lax.Precision.HIGHEST)
    kphi = total.reshape(NDOF, M).astype(jnp.bfloat16)
    return jnp.dot(modes.T, kphi, preferred_element_type=jnp.float32)
```

```python
import jax
import jax.numpy as jnp
from jax import lax
from jax.experimental import pallas as pl
from jax.experimental.pallas import tpu as pltpu
from jax.sharding import PartitionSpec as P

MESH = pl.DeviceIdType.MESH
BS = 64
CH = 256
BPC = CH // BS
W = 256
F32 = jnp.float32
BF16 = jnp.bfloat16

O, U, D, Q = (0, 0), (0, 1), (0, 3), (1, 1)
PAIRS = ((O, O), (O, Q), (U, O), (U, Q), (D, O), (D, Q), (D, U), (Q, O))


def kernel(
    modes, stiff, offs, out,
    own, kv, up, dn, qp, halo, ring, kphi, acc, xr, sb, fr,
    lsem, yu_s, yu_r, yd_s, yd_r, xq_s, xq_r, h_s, h_r, c_s, c_r, f_s, f_r,
):
    s, b = lax.axis_index("slab"), lax.axis_index("blk")
    z, xl, core = s // 4, (s // 2) % 2, s % 2
    xh, y = b // 4, b % 4
    nch = modes.shape[0] // CH
    slabs = lax.axis_size("slab")

    def blk_at(d):
        return ((xh + d[0]) % 2) * 4 + (y + d[1]) % 4

    outer = lax.rem(s + 2 * core - 1 + slabs, slabs)
    inner = s + 1 - 2 * core
    y_up, y_dn, x_far = (s, blk_at((0, 1))), (s, blk_at((0, 3))), (s, blk_at((1, 0)))
    across, beyond = (inner, b), (outer, b)

    def chunk(t):
        return t * core + (nch - 1 - t) * (1 - core)

    def rows(t):
        return pl.ds(pl.multiple_of(chunk(t) * CH, CH), CH)

    way = 2 * core - 1

    def site_of():
        dx, dy = (z // 4 + xh) % 2, (z % 4 + 4 - y) % 4
        bx, by = jnp.int32(0), jnp.int32(0)
        for r, c in PAIRS:
            hit = jnp.logical_and(dx == (c[0] - r[0]) % 2, dy == (c[1] - r[1]) % 4).astype(jnp.int32)
            bx = bx + hit * ((xh + r[0]) % 2)
            by = by + hit * ((y + 4 - r[1]) % 4)
        return bx * 4 + by

    site = site_of()
    mine = z * 2 + xl
    to_self = (site == b).astype(jnp.int32)

    copy_k = pltpu.make_async_copy(stiff, kv, lsem.at[0])
    copy_o = pltpu.make_async_copy(modes, own, lsem.at[1])
    copy_k.start()
    copy_o.start()

    barrier = pltpu.get_barrier_semaphore()
    for dev in (y_up, y_dn, x_far, across, beyond):
        pl.semaphore_signal(barrier, inc=1, device_id=dev, device_id_type=MESH)

    @pl.loop(0, 16)
    def _(i):
        @pl.when(jnp.logical_or(to_self == 0, i != mine))
        def _():
            pl.semaphore_signal(barrier, inc=1, device_id=(i * 2 + core, site), device_id_type=MESH)

    pl.semaphore_wait(barrier, 5 + 16 - to_self)

    def remote(src, dst, ssem, rsem, dev):
        return pltpu.make_async_remote_copy(src, dst, ssem, rsem, device_id=dev, device_id_type=MESH)

    def send_u(t):
        return remote(modes.at[rows(t)], up.at[rows(t)], yu_s.at[t], yu_r.at[t], y_dn)

    def send_d(t):
        return remote(modes.at[rows(t)], dn.at[rows(t)], yd_s.at[t], yd_r.at[t], y_up)

    def send_q(t):
        return remote(up.at[rows(t)], qp.at[rows(t)], xq_s.at[t], xq_r.at[t], x_far)

    ho_out = remote(modes.at[rows(nch - 1)], halo.at[0, 1], h_s.at[0], h_r.at[0], beyond)
    ho_in = remote(modes.at[rows(0)], halo.at[0, 0], h_s.at[1], h_r.at[1], across)
    hu_out = remote(halo.at[0, 1], halo.at[2, 1], h_s.at[2], h_r.at[2], y_dn)
    hu_in = remote(up.at[rows(0)], halo.at[2, 0], h_s.at[3], h_r.at[3], across)
    hq_out = remote(halo.at[2, 1], halo.at[1, 1], h_s.at[4], h_r.at[4], x_far)
    hq_in = remote(qp.at[rows(0)], halo.at[1, 0], h_s.at[5], h_r.at[5], across)

    ho_out.start()
    ho_in.start()

    @pl.loop(0, nch)
    def _(t):
        send_u(t).start()
        send_d(t).start()

    acc[...] = jnp.zeros_like(acc)
    copy_k.wait()
    copy_o.wait()
    ho_out.wait_recv()
    hu_out.start()

    def fill(slot, parts):
        for p, part in enumerate(parts):
            ring[pl.ds(slot * BPC, BPC), :, p * W:(p + 1) * W] = part.reshape(BPC, BS, W)

    def compute(j):
        c = chunk(j)
        for i in range(BPC):
            line = c * BPC + i
            where = []
            for col in range(8):
                pos = offs[line, col] + i
                slot = (j + 1 + way * (pos >> 2)) & 3
                where.append(slot * BPC + (pos & 3))
            lhs = kv[pl.ds(pl.multiple_of(line * BS, BS), BS), :]
            for p in range(3):
                gathered = jnp.concatenate([ring[w, :, p * W:(p + 1) * W] for w in where], axis=0)
                kphi[i * BS:(i + 1) * BS, p * W:(p + 1) * W] = jnp.dot(
                    lhs, gathered, preferred_element_type=F32
                ).astype(BF16)
        first = 0
        for ref, n in ((own, 2), (up, 2), (dn, 3), (qp, 1)):
            prod = lax.dot_general(
                kphi[:, : n * W], ref[rows(j), :], (((0,), (0,)), ((), ())), preferred_element_type=F32
            )
            acc[first:first + n] += prod.reshape(n, 2, 2, BS, W)
            first += n

    lag = 2

    @pl.loop(0, nch + lag + 1)
    def _(t):
        @pl.when(t < nch)
        def _():
            send_u(t).wait_recv()
            send_q(t).start()

        @pl.when(t == 0)
        def _():
            hu_in.start()

        @pl.when(t == 2)
        def _():
            hu_out.wait_recv()
            hq_out.start()

        j = t - lag

        @pl.when(j == 0)
        def _():
            send_q(0).wait_recv()
            hq_in.start()
            hu_in.wait_recv()
            ho_in.wait_recv()
            hq_in.wait_recv()
            fill(0, (halo[0, 0], halo[1, 0], halo[2, 0]))

        @pl.when(jnp.logical_and(j >= 0, j < nch))
        def _():
            @pl.when(j > 0)
            def _():
                send_q(j).wait_recv()

            fill((j + 1) & 3, (own[rows(j), :], qp[rows(j), :], up[rows(j), :]))

        @pl.when(j == nch)
        def _():
            hq_out.wait_recv()
            inside = jnp.logical_and(s + core > 0, s + core < slabs).astype(F32)
            fill(
                (nch + 1) & 3,
                [jnp.where(inside > 0, halo[p, 1], jnp.zeros((CH, W), BF16)) for p in range(3)],
            )

        @pl.when(j >= 1)
        def _():
            send_d(j - 1).wait_recv()
            compute(j - 1)

    def swap(p):
        return remote(acc.at[p, :, 1 - core], xr.at[p], c_s.at[p], c_r.at[p], across)

    for p in range(8):
        swap(p).start()

    def final(p, h):
        r, c = PAIRS[p]
        dev = ((((xh + c[0]) % 2) * 4 + (y + c[1]) % 4) * 4 + h * 2 + core, blk_at(r))
        return remote(sb.at[p, h], fr.at[mine], f_s.at[p, h], f_r.at[mine], dev), dev

    def is_self(p, h, dev):
        return jnp.logical_and(dev[0] == s, dev[1] == b)

    for p in range(8):
        swap(p).wait_recv()
        sb[p] = (acc[p, :, core] + xr[p]).astype(BF16)
        for h in range(2):
            cp, dev = final(p, h)
            if PAIRS[p][0] == O:
                @pl.when(is_self(p, h, dev))
                def _():
                    fr[mine] = sb[p, h]

                @pl.when(jnp.logical_not(is_self(p, h, dev)))
                def _():
                    cp.start()
            else:
                cp.start()

    total = jnp.zeros((BS, W), F32)
    out[...] = total

    @pl.loop(0, 16)
    def _(i):
        @pl.when(jnp.logical_or(to_self == 0, i != mine))
        def _():
            remote(sb.at[0, 0], fr.at[i], f_s.at[0, 0], f_r.at[i], across).wait_recv()

        out[...] += fr[i].astype(F32)

    for cp in (ho_out, ho_in, hu_out, hu_in, hq_out, hq_in):
        cp.wait_send()

    @pl.loop(0, nch)
    def _(t):
        send_u(t).wait_send()
        send_d(t).wait_send()
        send_q(t).wait_send()

    for p in range(8):
        swap(p).wait_send()
        for h in range(2):
            cp, dev = final(p, h)
            if PAIRS[p][0] == O:
                @pl.when(jnp.logical_not(is_self(p, h, dev)))
                def _():
                    cp.wait_send()
            else:
                cp.wait_send()


def body(modes, stiffness, offsets):
    n, w = modes.shape
    nch = n // CH
    dma = pltpu.SemaphoreType.DMA
    res = pl.pallas_call(
        kernel,
        out_shape=jax.ShapeDtypeStruct((BS, W), F32),
        in_specs=[
            pl.BlockSpec(memory_space=pl.ANY),
            pl.BlockSpec(memory_space=pl.ANY),
            pl.BlockSpec(memory_space=pltpu.SMEM),
        ],
        out_specs=pl.BlockSpec(memory_space=pltpu.VMEM),
        scratch_shapes=[
            pltpu.VMEM((n, w), BF16),
            pltpu.VMEM((n, 8 * BS), BF16),
            pltpu.VMEM((n, w), BF16),
            pltpu.VMEM((n, w), BF16),
            pltpu.VMEM((n, w), BF16),
            pltpu.VMEM((3, 2, CH, w), BF16),
            pltpu.VMEM((4 * BPC, BS, 3 * W), BF16),
            pltpu.VMEM((CH, 3 * W), BF16),
            pltpu.VMEM((8, 2, 2, BS, W), F32),
            pltpu.VMEM((8, 2, BS, W), F32),
            pltpu.VMEM((8, 2, BS, W), BF16),
            pltpu.VMEM((16, BS, W), BF16),
            dma((2,)),
            dma((nch,)), dma((nch,)), dma((nch,)), dma((nch,)), dma((nch,)), dma((nch,)),
            dma((6,)), dma((6,)), dma((8,)), dma((8,)), dma((8, 2)), dma((16,)),
        ],
        compiler_params=pltpu.CompilerParams(
            collective_id=0, has_side_effects=True, vmem_limit_bytes=60 * 2**20
        ),
    )(modes, stiffness, offsets)
    return res.T


def solution(mesh):
    in_specs = (P("slab", "blk"), P("slab", None), P("slab", None))
    return jax.shard_map(body, mesh=mesh, in_specs=in_specs, out_specs=P("blk", "slab"), check_vma=False)
```

```python
import jax
import jax.numpy as jnp
from jax import lax
from jax.experimental import pallas as pl
from jax.experimental.pallas import tpu as pltpu
from jax.sharding import PartitionSpec as P

MESH = pl.DeviceIdType.MESH
BS = 64
CH = 256
BPC = CH // BS
W = 256
F32 = jnp.float32
BF16 = jnp.bfloat16

O, U, D, Q = (0, 0), (0, 1), (0, 3), (1, 3)
PAIRS = ((O, O), (O, Q), (U, O), (U, Q), (D, O), (D, Q), (D, U), (Q, O))
SHIFT = (0, 2, 7, 3, 5, 4, 1, 6)
ORDER = (5, 3, 4, 1, 7, 2, 6, 0)
AHEAD = 3


def kernel(
    modes, stiff, offs, out,
    own, kv, up, dn, qp, halo, hmid, ring, kphi, acc, xr, sb, fr, fin,
    lsem, yu_s, yu_r, yd_s, yd_r, xq_s, xq_r, h_s, h_r, c_s, c_r, f_s, f_r, e_s, e_r,
):
    s, b = lax.axis_index("slab"), lax.axis_index("blk")
    z, xl, core = s // 4, (s // 2) % 2, s % 2
    xh, y = b // 4, b % 4
    nch = modes.shape[0] // CH
    slabs = lax.axis_size("slab")

    def blk_at(d):
        return ((xh + d[0]) % 2) * 4 + (y + d[1]) % 4

    outer = lax.rem(s + 2 * core - 1 + slabs, slabs)
    inner = s + 1 - 2 * core
    y_up, y_dn, x_far = (s, blk_at((0, 1))), (s, blk_at((0, 3))), (s, blk_at((1, 0)))
    across, beyond = (inner, b), (outer, b)

    def chunk(t):
        return t * core + (nch - 1 - t) * (1 - core)

    def rows(t):
        return pl.ds(pl.multiple_of(chunk(t) * CH, CH), CH)

    way = 2 * core - 1

    aside = (outer, blk_at((1, 0)))

    def pick(hit, values):
        return sum(jnp.where(hit(p), values(p), 0) for p in range(8))

    def added(p):
        return (b + SHIFT[p]) % 8 == z

    goal = (
        pick(added, lambda p: blk_at(PAIRS[p][1])) * 4 + xl * 2 + core,
        pick(added, lambda p: blk_at(PAIRS[p][0])),
    )

    def wanted(p):
        r, c = PAIRS[p]
        dx, dy = (c[0] - r[0]) % 2, (c[1] - r[1]) % 4
        return ((xh + dx) % 2) * 4 + (y + dy) % 4 == z

    def site(p):
        r, _ = PAIRS[p]
        return blk_at(((-r[0]) % 2, (-r[1]) % 4))

    origin = (
        pick(wanted, lambda p: (site(p) + SHIFT[p]) % 8) * 4 + xl * 2 + core,
        pick(wanted, site),
    )
    mine = z * 2 + xl
    moves = (z != b).astype(jnp.int32)

    copy_k = pltpu.make_async_copy(stiff, kv, lsem.at[0])
    copy_o = pltpu.make_async_copy(modes, own, lsem.at[1])
    copy_k.start()
    copy_o.start()

    barrier = pltpu.get_barrier_semaphore()
    for dev in (y_up, y_dn, x_far, across, beyond, aside):
        pl.semaphore_signal(barrier, inc=1, device_id=dev, device_id_type=MESH)

    @pl.loop(0, 16)
    def _(i):
        @pl.when(i != mine)
        def _():
            pl.semaphore_signal(barrier, inc=1, device_id=(i * 2 + core, b), device_id_type=MESH)

    @pl.when(moves > 0)
    def _():
        pl.semaphore_signal(barrier, inc=1, device_id=origin, device_id_type=MESH)

    pl.semaphore_wait(barrier, 6 + 15 + moves)

    def remote(src, dst, ssem, rsem, dev):
        return pltpu.make_async_remote_copy(src, dst, ssem, rsem, device_id=dev, device_id_type=MESH)

    def send_u(t):
        return remote(modes.at[rows(t)], up.at[rows(t)], yu_s.at[t], yu_r.at[t], y_dn)

    def send_d(t):
        return remote(modes.at[rows(t)], dn.at[rows(t)], yd_s.at[t], yd_r.at[t], y_up)

    def send_q(t):
        return remote(dn.at[rows(t)], qp.at[rows(t)], xq_s.at[t], xq_r.at[t], x_far)

    ho_out = remote(modes.at[rows(nch - 1)], halo.at[0, 1], h_s.at[0], h_r.at[0], beyond)
    ho_in = remote(modes.at[rows(0)], halo.at[0, 0], h_s.at[1], h_r.at[1], across)
    hu_out = remote(halo.at[0, 1], halo.at[2, 1], h_s.at[2], h_r.at[2], y_dn)
    hu_in = remote(up.at[rows(0)], halo.at[2, 0], h_s.at[3], h_r.at[3], across)
    hq_out = remote(hmid, halo.at[1, 1], h_s.at[4], h_r.at[4], y_up)
    hq_in = remote(qp.at[rows(0)], halo.at[1, 0], h_s.at[5], h_r.at[5], across)

    hx_out = remote(modes.at[rows(nch - 1)], hmid, h_s.at[6], h_r.at[6], aside)

    ho_out.start()
    hx_out.start()
    ho_in.start()

    @pl.loop(0, AHEAD)
    def _(t):
        send_u(t).start()
        send_d(t).start()

    acc[...] = jnp.zeros_like(acc)
    copy_k.wait()
    copy_o.wait()

    def fill(slot, parts):
        for p, part in enumerate(parts):
            ring[pl.ds(slot * BPC, BPC), :, p * W:(p + 1) * W] = part.reshape(BPC, BS, W)

    def compute(j):
        c = chunk(j)
        for i in range(BPC):
            line = c * BPC + i
            where = []
            for col in range(8):
                pos = offs[col, line] + i
                slot = (j + 1 + way * (pos >> 2)) & 3
                where.append(slot * BPC + (pos & 3))
            lhs = kv[pl.ds(pl.multiple_of(line * BS, BS), BS), :]
            for p in range(3):
                gathered = jnp.concatenate([ring[w, :, p * W:(p + 1) * W] for w in where], axis=0)
                kphi[i * BS:(i + 1) * BS, p * W:(p + 1) * W] = jnp.dot(
                    lhs, gathered, preferred_element_type=F32
                ).astype(BF16)
        first = 0
        for ref, n in ((own, 2), (up, 2), (dn, 3), (qp, 1)):
            prod = lax.dot_general(
                kphi[:, : n * W], ref[rows(j), :], (((0,), (0,)), ((), ())), preferred_element_type=F32
            )
            acc[first:first + n] += prod.reshape(n, 2, 2, BS, W)
            first += n

    lag = 2

    @pl.loop(0, nch + lag + 1)
    def _(t):
        @pl.when(t < nch)
        def _():
            send_d(t).wait_recv()
            send_q(t).start()

        @pl.when(t + AHEAD < nch)
        def _():
            send_u(t + AHEAD).start()
            send_d(t + AHEAD).start()

        @pl.when(t + AHEAD == nch)
        def _():
            ho_out.wait_recv()
            hu_out.start()
            hx_out.wait_recv()
            hq_out.start()

        j = t - lag

        @pl.when(j == 0)
        def _():
            send_u(0).wait_recv()
            hu_in.start()
            send_q(0).wait_recv()
            hq_in.start()
            hu_in.wait_recv()
            ho_in.wait_recv()
            hq_in.wait_recv()
            fill(0, (halo[0, 0], halo[1, 0], halo[2, 0]))

        @pl.when(jnp.logical_and(j >= 0, j < nch))
        def _():
            @pl.when(j > 0)
            def _():
                send_u(j).wait_recv()
                send_q(j).wait_recv()

            fill((j + 1) & 3, (own[rows(j), :], qp[rows(j), :], up[rows(j), :]))

        @pl.when(j == nch)
        def _():
            hu_out.wait_recv()
            hq_out.wait_recv()
            inside = jnp.logical_and(s + core > 0, s + core < slabs).astype(F32)
            fill(
                (nch + 1) & 3,
                [jnp.where(inside > 0, halo[p, 1], jnp.zeros((CH, W), BF16)) for p in range(3)],
            )

        @pl.when(j >= 1)
        def _():
            compute(j - 1)

    def swap(p):
        return remote(acc.at[p, :, 1 - core], xr.at[p], c_s.at[p], c_r.at[p], across)

    for p in ORDER:
        swap(p).start()

    def final(p, h):
        to = (b + SHIFT[p]) % 8
        dev = (to * 4 + h * 2 + core, b)
        return remote(sb.at[p, h], fr.at[mine], f_s.at[p, h], f_r.at[mine], dev), jnp.logical_and(to == z, h == xl)

    for p in ORDER:
        swap(p).wait_recv()
        sb[p] = (acc[p, :, core] + xr[p]).astype(BF16)
        for h in range(2):
            cp, stays = final(p, h)

            @pl.when(stays)
            def _():
                fr[mine] = sb[p, h]

            @pl.when(jnp.logical_not(stays))
            def _():
                cp.start()

    fin[0] = jnp.zeros((BS, W), F32)

    @pl.loop(0, 16)
    def _(i):
        @pl.when(i != mine)
        def _():
            remote(sb.at[0, 0], fr.at[i], f_s.at[0, 0], f_r.at[i], across).wait_recv()

        fin[0] += fr[i].astype(F32)

    home = remote(fin.at[0], fin.at[1], e_s, e_r, goal)

    @pl.when(moves > 0)
    def _():
        home.start()
        home.wait()
        out[...] = fin[1]

    @pl.when(moves == 0)
    def _():
        out[...] = fin[0]

    for cp in (ho_out, ho_in, hu_out, hu_in, hq_out, hq_in, hx_out):
        cp.wait_send()

    @pl.loop(0, nch)
    def _(t):
        send_u(t).wait_send()
        send_d(t).wait_send()
        send_q(t).wait_send()

    for p in range(8):
        swap(p).wait_send()
        for h in range(2):
            cp, stays = final(p, h)

            @pl.when(jnp.logical_not(stays))
            def _():
                cp.wait_send()


def body(modes, stiffness, offsets):
    n, w = modes.shape
    nch = n // CH
    dma = pltpu.SemaphoreType.DMA
    res = pl.pallas_call(
        kernel,
        out_shape=jax.ShapeDtypeStruct((BS, W), F32),
        in_specs=[
            pl.BlockSpec(memory_space=pl.ANY),
            pl.BlockSpec(memory_space=pl.ANY),
            pl.BlockSpec(memory_space=pltpu.SMEM),
        ],
        out_specs=pl.BlockSpec(memory_space=pltpu.VMEM),
        scratch_shapes=[
            pltpu.VMEM((n, w), BF16),
            pltpu.VMEM((n, 8 * BS), BF16),
            pltpu.VMEM((n, w), BF16),
            pltpu.VMEM((n, w), BF16),
            pltpu.VMEM((n, w), BF16),
            pltpu.VMEM((3, 2, CH, w), BF16),
            pltpu.VMEM((CH, w), BF16),
            pltpu.VMEM((4 * BPC, BS, 3 * W), BF16),
            pltpu.VMEM((CH, 3 * W), BF16),
            pltpu.VMEM((8, 2, 2, BS, W), F32),
            pltpu.VMEM((8, 2, BS, W), F32),
            pltpu.VMEM((8, 2, BS, W), BF16),
            pltpu.VMEM((16, BS, W), BF16),
            pltpu.VMEM((2, BS, W), F32),
            dma((2,)),
            dma((nch,)), dma((nch,)), dma((nch,)), dma((nch,)), dma((nch,)), dma((nch,)),
            dma((7,)), dma((7,)), dma((8,)), dma((8,)), dma((8, 2)), dma((16,)), dma, dma,
        ],
        compiler_params=pltpu.CompilerParams(
            collective_id=0, has_side_effects=True, vmem_limit_bytes=60 * 2**20
        ),
    )(modes, stiffness, offsets.T)
    return res.T


def solution(mesh):
    in_specs = (P("slab", "blk"), P("slab", None), P("slab", None))
    return jax.shard_map(body, mesh=mesh, in_specs=in_specs, out_specs=P("blk", "slab"), check_vma=False)
```

```python
import jax
import jax.numpy as jnp
from jax import lax
from jax.experimental import pallas as pl
from jax.experimental.pallas import tpu as pltpu
from jax.sharding import PartitionSpec as P

MESH = pl.DeviceIdType.MESH
BS = 64
CH = 256
BPC = CH // BS
W = 256
F32 = jnp.float32
BF16 = jnp.bfloat16

O, U, D, Q = (0, 0), (0, 1), (0, 3), (1, 3)
PAIRS = ((O, O), (O, Q), (U, O), (U, Q), (D, O), (D, Q), (D, U), (Q, O))
ORDER = (0, 4, 2, 7, 1, 5, 3, 6)
AHEAD = 3


def kernel(
    modes, stiff, offs, out,
    own, kv, up, dn, qp, halo, hmid, ring, kphi, acc, xr, sb, mid, fr,
    lsem, yu_s, yu_r, yd_s, yd_r, xq_s, xq_r, h_s, h_r, c_s, c_r, f_s, f_r, m_s, m_r, tok,
):
    s, b = lax.axis_index("slab"), lax.axis_index("blk")
    z, xl, core = s // 4, (s // 2) % 2, s % 2
    xh, y = b // 4, b % 4
    nch = modes.shape[0] // CH
    slabs = lax.axis_size("slab")

    def blk_at(d):
        return ((xh + d[0]) % 2) * 4 + (y + d[1]) % 4

    outer = lax.rem(s + 2 * core - 1 + slabs, slabs)
    inner = s + 1 - 2 * core
    y_up, y_dn, x_far = (s, blk_at((0, 1))), (s, blk_at((0, 3))), (s, blk_at((1, 0)))
    across, beyond = (inner, b), (outer, b)

    def chunk(t):
        return t * core + (nch - 1 - t) * (1 - core)

    def rows(t):
        return pl.ds(pl.multiple_of(chunk(t) * CH, CH), CH)

    way = 2 * core - 1

    aside = (outer, blk_at((1, 0)))

    z_up, z_dn = (lax.rem(s + 4, slabs), b), (lax.rem(s + slabs - 4, slabs), b)
    beside = (s + 2 - 4 * xl, b)
    mine = z * 2 + xl

    copy_k = pltpu.make_async_copy(stiff, kv, lsem.at[0])
    copy_o = pltpu.make_async_copy(modes, own, lsem.at[1])
    copy_k.start()
    copy_o.start()

    barrier = pltpu.get_barrier_semaphore()
    near = (y_up, y_dn, x_far, across, beyond, aside, (s, blk_at((1, 1))), z_up, z_dn, beside)
    for dev in near:
        pl.semaphore_signal(barrier, inc=1, device_id=dev, device_id_type=MESH)
    pl.semaphore_wait(barrier, len(near))

    def tell(k):
        if k < 3:
            pl.semaphore_signal(tok.at[2 * k], inc=1, device_id=z_up, device_id_type=MESH)
            pl.semaphore_signal(tok.at[2 * k + 1], inc=1, device_id=z_dn, device_id_type=MESH)
        else:
            pl.semaphore_signal(tok.at[6], inc=1, device_id=beside, device_id_type=MESH)

    def hear(k):
        if k < 3:
            pl.semaphore_wait(tok.at[2 * k], 1)
            pl.semaphore_wait(tok.at[2 * k + 1], 1)
        else:
            pl.semaphore_wait(tok.at[6], 1)

    def remote(src, dst, ssem, rsem, dev):
        return pltpu.make_async_remote_copy(src, dst, ssem, rsem, device_id=dev, device_id_type=MESH)

    def send_u(t):
        return remote(modes.at[rows(t)], up.at[rows(t)], yu_s.at[t], yu_r.at[t], y_dn)

    def send_d(t):
        return remote(modes.at[rows(t)], dn.at[rows(t)], yd_s.at[t], yd_r.at[t], y_up)

    def send_q(t):
        return remote(dn.at[rows(t)], qp.at[rows(t)], xq_s.at[t], xq_r.at[t], x_far)

    ho_out = remote(modes.at[rows(nch - 1)], halo.at[0, 1], h_s.at[0], h_r.at[0], beyond)
    ho_in = remote(modes.at[rows(0)], halo.at[0, 0], h_s.at[1], h_r.at[1], across)
    hu_out = remote(halo.at[0, 1], halo.at[2, 1], h_s.at[2], h_r.at[2], y_dn)
    hu_in = remote(up.at[rows(0)], halo.at[2, 0], h_s.at[3], h_r.at[3], across)
    hq_out = remote(hmid, halo.at[1, 1], h_s.at[4], h_r.at[4], y_up)
    hq_in = remote(qp.at[rows(0)], halo.at[1, 0], h_s.at[5], h_r.at[5], across)

    hx_out = remote(modes.at[rows(nch - 1)], hmid, h_s.at[6], h_r.at[6], aside)

    ho_out.start()
    hx_out.start()
    ho_in.start()

    @pl.loop(0, AHEAD)
    def _(t):
        send_u(t).start()
        send_d(t).start()

    acc[...] = jnp.zeros_like(acc)
    copy_k.wait()
    copy_o.wait()

    def fill(slot, parts):
        for p, part in enumerate(parts):
            ring[pl.ds(slot * BPC, BPC), :, p * W:(p + 1) * W] = part.reshape(BPC, BS, W)

    def compute(j):
        c = chunk(j)
        for i in range(BPC):
            line = c * BPC + i
            where = []
            for col in range(8):
                pos = offs[col, line] + i
                slot = (j + 1 + way * (pos >> 2)) & 3
                where.append(slot * BPC + (pos & 3))
            lhs = kv[pl.ds(pl.multiple_of(line * BS, BS), BS), :]
            for p in range(3):
                gathered = jnp.concatenate([ring[w, :, p * W:(p + 1) * W] for w in where], axis=0)
                kphi[i * BS:(i + 1) * BS, p * W:(p + 1) * W] = jnp.dot(
                    lhs, gathered, preferred_element_type=F32
                ).astype(BF16)
        first = 0
        for ref, n in ((own, 2), (up, 2), (dn, 3), (qp, 1)):
            prod = lax.dot_general(
                kphi[:, : n * W], ref[rows(j), :], (((0,), (0,)), ((), ())), preferred_element_type=F32
            )
            acc[first:first + n] += prod.reshape(n, 2, 2, BS, W)
            first += n

    lag = 2

    @pl.loop(0, nch + lag + 1)
    def _(t):
        @pl.when(t < nch)
        def _():
            send_d(t).wait_recv()
            send_q(t).start()

        @pl.when(t + AHEAD < nch)
        def _():
            send_u(t + AHEAD).start()
            send_d(t + AHEAD).start()

        @pl.when(t + AHEAD == nch)
        def _():
            ho_out.wait_recv()
            hu_out.start()
            hx_out.wait_recv()
            hq_out.start()

        for k in range(5):
            @pl.when(t == 2 * k + 2)
            def _():
                if k > 0:
                    hear(k - 1)
                if k < 4:
                    tell(k)

        j = t - lag

        @pl.when(j == 0)
        def _():
            send_u(0).wait_recv()
            hu_in.start()
            send_q(0).wait_recv()
            hq_in.start()
            hu_in.wait_recv()
            ho_in.wait_recv()
            hq_in.wait_recv()
            fill(0, (halo[0, 0], halo[1, 0], halo[2, 0]))

        @pl.when(jnp.logical_and(j >= 0, j < nch))
        def _():
            @pl.when(j > 0)
            def _():
                send_u(j).wait_recv()
                send_q(j).wait_recv()

            fill((j + 1) & 3, (own[rows(j), :], qp[rows(j), :], up[rows(j), :]))

        @pl.when(j == nch)
        def _():
            hu_out.wait_recv()
            hq_out.wait_recv()
            inside = jnp.logical_and(s + core > 0, s + core < slabs).astype(F32)
            fill(
                (nch + 1) & 3,
                [jnp.where(inside > 0, halo[p, 1], jnp.zeros((CH, W), BF16)) for p in range(3)],
            )

        @pl.when(j >= 1)
        def _():
            compute(j - 1)

    def swap(p):
        return remote(acc.at[p, :, 1 - core], xr.at[p], c_s.at[p], c_r.at[p], across)

    for p in ORDER:
        swap(p).start()

    def final(p, h):
        r, c = PAIRS[p]
        to = blk_at(((c[0] - r[0]) % 2, (c[1] - r[1]) % 4))
        piece = sb.at[p, h] if r == O else mid.at[p, h]
        cp = remote(piece, fr.at[mine], f_s.at[p, h], f_r.at[mine], (to * 4 + h * 2 + core, b))
        return cp, piece, jnp.logical_and(to == z, h == xl)

    def move(p):
        return remote(sb.at[p], mid.at[p], m_s.at[p], m_r.at[p], (s, blk_at(PAIRS[p][0])))

    def settle(p):
        for h in range(2):
            cp, piece, stays = final(p, h)

            @pl.when(stays)
            def _():
                fr[mine] = piece[...]

            @pl.when(jnp.logical_not(stays))
            def _():
                cp.start()

    for p in ORDER:
        swap(p).wait_recv()
        sb[p] = (acc[p, :, core] + xr[p]).astype(BF16)
        if PAIRS[p][0] == O:
            settle(p)
        else:
            move(p).start()
    for p in ORDER:
        if PAIRS[p][0] != O:
            move(p).wait_recv()
            settle(p)

    out[...] = jnp.zeros((BS, W), F32)

    @pl.loop(0, 16)
    def _(i):
        @pl.when(i != mine)
        def _():
            remote(sb.at[0, 0], fr.at[i], f_s.at[0, 0], f_r.at[i], across).wait_recv()

        out[...] += fr[i].astype(F32)

    for cp in (ho_out, ho_in, hu_out, hu_in, hq_out, hq_in, hx_out):
        cp.wait_send()

    @pl.loop(0, nch)
    def _(t):
        send_u(t).wait_send()
        send_d(t).wait_send()
        send_q(t).wait_send()

    for p in range(8):
        swap(p).wait_send()
        if PAIRS[p][0] != O:
            move(p).wait_send()
        for h in range(2):
            cp, _, stays = final(p, h)

            @pl.when(jnp.logical_not(stays))
            def _():
                cp.wait_send()


def body(modes, stiffness, offsets):
    n, w = modes.shape
    nch = n // CH
    dma = pltpu.SemaphoreType.DMA
    res = pl.pallas_call(
        kernel,
        out_shape=jax.ShapeDtypeStruct((BS, W), F32),
        in_specs=[
            pl.BlockSpec(memory_space=pl.ANY),
            pl.BlockSpec(memory_space=pl.ANY),
            pl.BlockSpec(memory_space=pltpu.SMEM),
        ],
        out_specs=pl.BlockSpec(memory_space=pltpu.VMEM),
        scratch_shapes=[
            pltpu.VMEM((n, w), BF16),
            pltpu.VMEM((n, 8 * BS), BF16),
            pltpu.VMEM((n, w), BF16),
            pltpu.VMEM((n, w), BF16),
            pltpu.VMEM((n, w), BF16),
            pltpu.VMEM((3, 2, CH, w), BF16),
            pltpu.VMEM((CH, w), BF16),
            pltpu.VMEM((4 * BPC, BS, 3 * W), BF16),
            pltpu.VMEM((CH, 3 * W), BF16),
            pltpu.VMEM((8, 2, 2, BS, W), F32),
            pltpu.VMEM((8, 2, BS, W), F32),
            pltpu.VMEM((8, 2, BS, W), BF16),
            pltpu.VMEM((8, 2, BS, W), BF16),
            pltpu.VMEM((16, BS, W), BF16),
            dma((2,)),
            dma((nch,)), dma((nch,)), dma((nch,)), dma((nch,)), dma((nch,)), dma((nch,)),
            dma((7,)), dma((7,)), dma((8,)), dma((8,)), dma((8, 2)), dma((16,)), dma((8,)), dma((8,)),
            pltpu.SemaphoreType.REGULAR((7,)),
        ],
        compiler_params=pltpu.CompilerParams(
            collective_id=0, has_side_effects=True, vmem_limit_bytes=60 * 2**20
        ),
    )(modes, stiffness, offsets.T)
    return res.T


def solution(mesh):
    in_specs = (P("slab", "blk"), P("slab", None), P("slab", None))
    return jax.shard_map(body, mesh=mesh, in_specs=in_specs, out_specs=P("blk", "slab"), check_vma=False)
```

```python
import jax
import jax.numpy as jnp
from jax import lax
from jax.experimental import pallas as pl
from jax.experimental.pallas import tpu as pltpu
from jax.sharding import PartitionSpec as P

MESH = pl.DeviceIdType.MESH
BS = 64
CH = 256
BPC = CH // BS
W = 256
F32 = jnp.float32
BF16 = jnp.bfloat16

O, U, D, Q = (0, 0), (0, 1), (0, 3), (1, 3)
PAIRS = ((O, O), (O, Q), (U, O), (U, Q), (D, O), (D, Q), (D, U), (Q, O))
EARLY = (2, 4, 0)
STEPS = (
    (2, True), (4, True), (7, False), (5, False), (3, False), (6, False), (1, False),
    (7, True), (5, True), (3, True), (6, True),
)
AHEAD = 3


def kernel(
    modes, stiff, offsets, out,
    offs, own, kv, up, dn, qp, halo, hmid, ring_o, ring, kphi_o, kphi, acc, xr, sb, mid, fr,
    lsem, yu_s, yu_r, yd_s, yd_r, xq_s, xq_r, h_s, h_r, c_s, c_r, f_s, f_r, m_s, m_r, tok,
):
    s, b = lax.axis_index("slab"), lax.axis_index("blk")
    z, xl, core = s // 4, (s // 2) % 2, s % 2
    xh, y = b // 4, b % 4
    nch = modes.shape[0] // CH
    slabs = lax.axis_size("slab")

    def blk_at(d):
        return ((xh + d[0]) % 2) * 4 + (y + d[1]) % 4

    outer = lax.rem(s + 2 * core - 1 + slabs, slabs)
    inner = s + 1 - 2 * core
    y_up, y_dn, x_far = (s, blk_at((0, 1))), (s, blk_at((0, 3))), (s, blk_at((1, 0)))
    across, beyond = (inner, b), (outer, b)

    def chunk(t):
        return t * core + (nch - 1 - t) * (1 - core)

    def rows(t):
        return pl.ds(pl.multiple_of(chunk(t) * CH, CH), CH)

    way = 2 * core - 1

    aside = (outer, blk_at((1, 0)))

    z_up, z_dn = (lax.rem(s + 4, slabs), b), (lax.rem(s + slabs - 4, slabs), b)
    beside = (s + 2 - 4 * xl, b)
    mine = z * 2 + xl

    copy_k = pltpu.make_async_copy(stiff, kv, lsem.at[0])
    copy_o = pltpu.make_async_copy(modes, own, lsem.at[1])
    copy_f = pltpu.make_async_copy(offsets, offs, lsem.at[2])
    copy_f.start()
    copy_k.start()
    copy_o.start()

    barrier = pltpu.get_barrier_semaphore()
    near = (y_up, y_dn, x_far, across, beyond, aside, (s, blk_at((1, 1))), z_up, z_dn, beside)
    for dev in near:
        pl.semaphore_signal(barrier, inc=1, device_id=dev, device_id_type=MESH)
    pl.semaphore_wait(barrier, len(near))

    def tell(k):
        if k < 3:
            pl.semaphore_signal(tok.at[2 * k], inc=1, device_id=z_up, device_id_type=MESH)
            pl.semaphore_signal(tok.at[2 * k + 1], inc=1, device_id=z_dn, device_id_type=MESH)
        else:
            pl.semaphore_signal(tok.at[6], inc=1, device_id=beside, device_id_type=MESH)

    def hear(k):
        if k < 3:
            pl.semaphore_wait(tok.at[2 * k], 1)
            pl.semaphore_wait(tok.at[2 * k + 1], 1)
        else:
            pl.semaphore_wait(tok.at[6], 1)

    def remote(src, dst, ssem, rsem, dev):
        return pltpu.make_async_remote_copy(src, dst, ssem, rsem, device_id=dev, device_id_type=MESH)

    def send_u(t):
        return remote(modes.at[rows(t)], up.at[rows(t)], yu_s.at[t], yu_r.at[t], y_dn)

    def send_d(t):
        return remote(modes.at[rows(t)], dn.at[rows(t)], yd_s.at[t], yd_r.at[t], y_up)

    def send_q(t):
        return remote(dn.at[rows(t)], qp.at[rows(t)], xq_s.at[t], xq_r.at[t], x_far)

    ho_out = remote(modes.at[rows(nch - 1)], halo.at[0, 1], h_s.at[0], h_r.at[0], beyond)
    ho_in = remote(modes.at[rows(0)], halo.at[0, 0], h_s.at[1], h_r.at[1], across)
    hu_out = remote(halo.at[0, 1], halo.at[2, 1], h_s.at[2], h_r.at[2], y_dn)
    hu_in = remote(up.at[rows(0)], halo.at[2, 0], h_s.at[3], h_r.at[3], across)
    hq_out = remote(hmid, halo.at[1, 1], h_s.at[4], h_r.at[4], y_up)
    hq_in = remote(qp.at[rows(0)], halo.at[1, 0], h_s.at[5], h_r.at[5], across)

    hx_out = remote(modes.at[rows(nch - 1)], hmid, h_s.at[6], h_r.at[6], aside)

    ho_out.start()
    hx_out.start()
    ho_in.start()

    @pl.loop(0, AHEAD)
    def _(t):
        send_u(t).start()
        send_d(t).start()

    acc[...] = jnp.zeros_like(acc)
    copy_f.wait()
    copy_k.wait()
    copy_o.wait()

    def fill(ref, slot, parts):
        for p, part in enumerate(parts):
            ref[pl.ds(slot * BPC, BPC), :, p * W:(p + 1) * W] = part.reshape(BPC, BS, W)

    def stage1(j, ref, panels, store):
        c = chunk(j)
        for i in range(BPC):
            line = c * BPC + i
            where = []
            for col in range(8):
                pos = offs[col, line] + i
                slot = (j + 1 + way * (pos >> 2)) & 3
                where.append(slot * BPC + (pos & 3))
            lhs = kv[pl.ds(pl.multiple_of(line * BS, BS), BS), :]
            for p in range(panels):
                gathered = jnp.concatenate([ref[w, :, p * W:(p + 1) * W] for w in where], axis=0)
                store(i, p, jnp.dot(lhs, gathered, preferred_element_type=F32).astype(BF16))

    def add(first, n, left, right):
        prod = lax.dot_general(left, right, (((0,), (0,)), ((), ())), preferred_element_type=F32)
        acc[first:first + n] += prod.reshape(n, 2, 2, BS, W)

    def early(j):
        base = chunk(j) * CH

        def store(i, p, value):
            kphi_o[pl.ds(pl.multiple_of(base + i * BS, BS), BS), :] = value

        stage1(j, ring_o, 1, store)
        for ref, p in ((up, 2), (dn, 4), (own, 0)):
            add(p, 1, kphi_o[rows(j), :], ref[rows(j), :])

    def late(j, done=None):
        def store(i, p, value):
            kphi[i * BS:(i + 1) * BS, p * W:(p + 1) * W] = value

        stage1(j, ring, 2, store)
        for first, n, left, right in (
            (7, 1, kphi_o[rows(j), :], qp), (5, 2, kphi[...], dn), (3, 1, kphi[:, :W], up), (1, 1, kphi[:, :W], own),
        ):
            add(first, n, left, right[rows(j), :])
            for p in range(first, first + n):
                if done is not None:
                    done(p)

    inside = jnp.logical_and(s + core > 0, s + core < slabs).astype(F32)

    def beyond_face(p):
        return jnp.where(inside > 0, halo[p, 1], jnp.zeros((CH, W), BF16))

    def swap(p):
        return remote(acc.at[p, :, 1 - core], xr.at[p], c_s.at[p], c_r.at[p], across)

    def final(p, h):
        r, c = PAIRS[p]
        to = blk_at(((c[0] - r[0]) % 2, (c[1] - r[1]) % 4))
        piece = sb.at[p, h] if r == O else mid.at[p, h]
        cp = remote(piece, fr.at[mine], f_s.at[p, h], f_r.at[mine], (to * 4 + h * 2 + core, b))
        return cp, piece, jnp.logical_and(to == z, h == xl)

    def move(p):
        return remote(sb.at[p], mid.at[p], m_s.at[p], m_r.at[p], (s, blk_at(PAIRS[p][0])))

    def settle(p):
        for h in range(2):
            cp, piece, stays = final(p, h)

            @pl.when(stays)
            def _():
                fr[mine] = piece[...]

            @pl.when(jnp.logical_not(stays))
            def _():
                cp.start()

    def leave(p):
        swap(p).wait_recv()
        sb[p] = (acc[p, :, core] + xr[p]).astype(BF16)
        if PAIRS[p][0] == O:
            settle(p)
        else:
            move(p).start()

    lag = 2

    @pl.loop(0, nch + lag)
    def _(t):
        @pl.when(t < nch)
        def _():
            send_d(t).wait_recv()
            send_q(t).start()

        @pl.when(t + AHEAD < nch)
        def _():
            send_u(t + AHEAD).start()
            send_d(t + AHEAD).start()

        @pl.when(t + AHEAD == nch)
        def _():
            ho_out.wait_recv()
            hu_out.start()
            hx_out.wait_recv()
            hq_out.start()

        for k in range(5):
            @pl.when(t == 2 * k + 2)
            def _():
                if k > 0:
                    hear(k - 1)
                if k < 4:
                    tell(k)

        @pl.when(t == 0)
        def _():
            ho_in.wait_recv()
            fill(ring_o, 0, (halo[0, 0],))

        @pl.when(t < nch)
        def _():
            fill(ring_o, (t + 1) & 3, (own[rows(t), :],))

        @pl.when(t == nch)
        def _():
            fill(ring_o, (nch + 1) & 3, (beyond_face(0),))

        @pl.when(jnp.logical_and(t >= 1, t <= nch))
        def _():
            send_u(t - 1).wait_recv()
            early(t - 1)

        @pl.when(t == nch)
        def _():
            for p in EARLY:
                swap(p).start()

        @pl.when(t == nch + 1)
        def _():
            for p in EARLY:
                leave(p)

        j = t - lag

        @pl.when(j == 0)
        def _():
            hu_in.start()
            send_q(0).wait_recv()
            hq_in.start()
            hu_in.wait_recv()
            hq_in.wait_recv()
            fill(ring, 0, (halo[1, 0], halo[2, 0]))

        @pl.when(j >= 0)
        def _():
            @pl.when(j > 0)
            def _():
                send_q(j).wait_recv()

            fill(ring, (j + 1) & 3, (qp[rows(j), :], up[rows(j), :]))

        @pl.when(j >= 1)
        def _():
            late(j - 1)

    hu_out.wait_recv()
    hq_out.wait_recv()
    fill(ring, (nch + 1) & 3, (beyond_face(1), beyond_face(2)))
    late(nch - 1, lambda p: swap(p).start())

    for p, arrived in STEPS:
        if arrived:
            move(p).wait_recv()
            settle(p)
        else:
            leave(p)

    out[...] = jnp.zeros((BS, W), F32)

    @pl.loop(0, 16)
    def _(i):
        @pl.when(i != mine)
        def _():
            remote(sb.at[0, 0], fr.at[i], f_s.at[0, 0], f_r.at[i], across).wait_recv()

        out[...] += fr[i].astype(F32)

    for cp in (ho_out, ho_in, hu_out, hu_in, hq_out, hq_in, hx_out):
        cp.wait_send()

    @pl.loop(0, nch)
    def _(t):
        send_u(t).wait_send()
        send_d(t).wait_send()
        send_q(t).wait_send()

    for p in range(8):
        swap(p).wait_send()
        if PAIRS[p][0] != O:
            move(p).wait_send()
        for h in range(2):
            cp, _, stays = final(p, h)

            @pl.when(jnp.logical_not(stays))
            def _():
                cp.wait_send()


def body(modes, stiffness, offsets):
    n, w = modes.shape
    nch = n // CH
    dma = pltpu.SemaphoreType.DMA
    res = pl.pallas_call(
        kernel,
        out_shape=jax.ShapeDtypeStruct((BS, W), F32),
        in_specs=[
            pl.BlockSpec(memory_space=pl.ANY),
            pl.BlockSpec(memory_space=pl.ANY),
            pl.BlockSpec(memory_space=pl.ANY),
        ],
        out_specs=pl.BlockSpec(memory_space=pltpu.VMEM),
        scratch_shapes=[
            pltpu.SMEM(offsets.shape[::-1], jnp.int32),
            pltpu.VMEM((n, w), BF16),
            pltpu.VMEM((n, 8 * BS), BF16),
            pltpu.VMEM((n, w), BF16),
            pltpu.VMEM((n, w), BF16),
            pltpu.VMEM((n, w), BF16),
            pltpu.VMEM((3, 2, CH, w), BF16),
            pltpu.VMEM((CH, w), BF16),
            pltpu.VMEM((4 * BPC, BS, W), BF16),
            pltpu.VMEM((4 * BPC, BS, 2 * W), BF16),
            pltpu.VMEM((n, W), BF16),
            pltpu.VMEM((CH, 2 * W), BF16),
            pltpu.VMEM((8, 2, 2, BS, W), F32),
            pltpu.VMEM((8, 2, BS, W), F32),
            pltpu.VMEM((8, 2, BS, W), BF16),
            pltpu.VMEM((8, 2, BS, W), BF16),
            pltpu.VMEM((16, BS, W), BF16),
            dma((3,)),
            dma((nch,)), dma((nch,)), dma((nch,)), dma((nch,)), dma((nch,)), dma((nch,)),
            dma((7,)), dma((7,)), dma((8,)), dma((8,)), dma((8, 2)), dma((16,)), dma((8,)), dma((8,)),
            pltpu.SemaphoreType.REGULAR((7,)),
        ],
        compiler_params=pltpu.CompilerParams(
            collective_id=0, has_side_effects=True, vmem_limit_bytes=60 * 2**20
        ),
    )(modes, stiffness, offsets.T)
    return res.T


def solution(mesh):
    in_specs = (P("slab", "blk"), P("slab", None), P("slab", None))
    return jax.shard_map(body, mesh=mesh, in_specs=in_specs, out_specs=P("blk", "slab"), check_vma=False)
```

```python
import jax
import jax.numpy as jnp
from jax import lax
from jax.experimental import pallas as pl
from jax.experimental.pallas import tpu as pltpu
from jax.sharding import PartitionSpec as P

MESH = pl.DeviceIdType.MESH
BS = 64
CH = 256
BPC = CH // BS
W = 256
F32 = jnp.float32
BF16 = jnp.bfloat16

O, U, D, Q = (0, 0), (0, 1), (0, 3), (1, 3)
PAIRS = ((O, O), (O, Q), (O, U), (U, O), (U, Q), (D, Q), (D, U), (Q, O))
EARLY = (3, 0)
STEPS = (
    (3, True), (5, False), (4, False), (7, False), (6, False), (1, False), (2, False),
    (5, True), (4, True), (7, True), (6, True),
)
AHEAD = 3


def kernel(
    modes, stiff, offsets, out,
    offs, own, kv, up, dn, qp, halo, hmid, ring_o, ring, kphi_o, kphi, acc, xr, sb, mid, fr,
    lsem, yu_s, yu_r, yd_s, yd_r, xq_s, xq_r, h_s, h_r, c_s, c_r, f_s, f_r, m_s, m_r, tok,
):
    s, b = lax.axis_index("slab"), lax.axis_index("blk")
    z, xl, core = s // 4, (s // 2) % 2, s % 2
    xh, y = b // 4, b % 4
    nch = modes.shape[0] // CH
    slabs = lax.axis_size("slab")

    def blk_at(d):
        return ((xh + d[0]) % 2) * 4 + (y + d[1]) % 4

    outer = lax.rem(s + 2 * core - 1 + slabs, slabs)
    inner = s + 1 - 2 * core
    y_up, y_dn, x_far = (s, blk_at((0, 1))), (s, blk_at((0, 3))), (s, blk_at((1, 0)))
    across, beyond = (inner, b), (outer, b)

    def chunk(t):
        return t * core + (nch - 1 - t) * (1 - core)

    def rows(t):
        return pl.ds(pl.multiple_of(chunk(t) * CH, CH), CH)

    way = 2 * core - 1

    aside = (outer, blk_at((1, 0)))

    z_up, z_dn = (lax.rem(s + 4, slabs), b), (lax.rem(s + slabs - 4, slabs), b)
    beside = (s + 2 - 4 * xl, b)
    mine = z * 2 + xl

    copy_k = pltpu.make_async_copy(stiff, kv, lsem.at[0])
    copy_o = pltpu.make_async_copy(modes, own, lsem.at[1])
    copy_f = pltpu.make_async_copy(offsets, offs, lsem.at[2])
    copy_f.start()
    copy_k.start()
    copy_o.start()

    barrier = pltpu.get_barrier_semaphore()
    near = (y_up, y_dn, x_far, across, beyond, aside, (s, blk_at((1, 1))), z_up, z_dn, beside)
    for dev in near:
        pl.semaphore_signal(barrier, inc=1, device_id=dev, device_id_type=MESH)
    pl.semaphore_wait(barrier, len(near))

    def tell(k):
        if k < 3:
            pl.semaphore_signal(tok.at[2 * k], inc=1, device_id=z_up, device_id_type=MESH)
            pl.semaphore_signal(tok.at[2 * k + 1], inc=1, device_id=z_dn, device_id_type=MESH)
        else:
            pl.semaphore_signal(tok.at[6], inc=1, device_id=beside, device_id_type=MESH)

    def hear(k):
        if k < 3:
            pl.semaphore_wait(tok.at[2 * k], 1)
            pl.semaphore_wait(tok.at[2 * k + 1], 1)
        else:
            pl.semaphore_wait(tok.at[6], 1)

    def remote(src, dst, ssem, rsem, dev):
        return pltpu.make_async_remote_copy(src, dst, ssem, rsem, device_id=dev, device_id_type=MESH)

    def send_u(t):
        return remote(modes.at[rows(t)], up.at[rows(t)], yu_s.at[t], yu_r.at[t], y_dn)

    def send_d(t):
        return remote(modes.at[rows(t)], dn.at[rows(t)], yd_s.at[t], yd_r.at[t], y_up)

    def send_q(t):
        return remote(dn.at[rows(t)], qp.at[rows(t)], xq_s.at[t], xq_r.at[t], x_far)

    ho_out = remote(modes.at[rows(nch - 1)], halo.at[0, 1], h_s.at[0], h_r.at[0], beyond)
    ho_in = remote(modes.at[rows(0)], halo.at[0, 0], h_s.at[1], h_r.at[1], across)
    hu_out = remote(halo.at[0, 1], halo.at[2, 1], h_s.at[2], h_r.at[2], y_dn)
    hu_in = remote(up.at[rows(0)], halo.at[2, 0], h_s.at[3], h_r.at[3], across)
    hq_out = remote(hmid, halo.at[1, 1], h_s.at[4], h_r.at[4], y_up)
    hq_in = remote(qp.at[rows(0)], halo.at[1, 0], h_s.at[5], h_r.at[5], across)

    hx_out = remote(modes.at[rows(nch - 1)], hmid, h_s.at[6], h_r.at[6], aside)

    ho_out.start()
    hx_out.start()
    ho_in.start()

    @pl.loop(0, AHEAD)
    def _(t):
        send_u(t).start()
        send_d(t).start()

    acc[...] = jnp.zeros_like(acc)
    copy_f.wait()
    copy_k.wait()
    copy_o.wait()

    def fill(ref, slot, parts):
        for p, part in enumerate(parts):
            ref[pl.ds(slot * BPC, BPC), :, p * W:(p + 1) * W] = part.reshape(BPC, BS, W)

    def stage1(j, ref, panels, store):
        c = chunk(j)
        for i in range(BPC):
            line = c * BPC + i
            where = []
            for col in range(8):
                pos = offs[col, line] + i
                slot = (j + 1 + way * (pos >> 2)) & 3
                where.append(slot * BPC + (pos & 3))
            lhs = kv[pl.ds(pl.multiple_of(line * BS, BS), BS), :]
            for p in range(panels):
                gathered = jnp.concatenate([ref[w, :, p * W:(p + 1) * W] for w in where], axis=0)
                store(i, p, jnp.dot(lhs, gathered, preferred_element_type=F32).astype(BF16))

    def add(first, n, left, right):
        prod = lax.dot_general(left, right, (((0,), (0,)), ((), ())), preferred_element_type=F32)
        acc[first:first + n] += prod.reshape(n, 2, 2, BS, W)

    def early(j):
        base = chunk(j) * CH

        def store(i, p, value):
            kphi_o[pl.ds(pl.multiple_of(base + i * BS, BS), BS), :] = value

        stage1(j, ring_o, 1, store)
        for ref, p in ((up, 3), (own, 0)):
            add(p, 1, kphi_o[rows(j), :], ref[rows(j), :])

    def late(j, done=None):
        def store(i, p, value):
            kphi[i * BS:(i + 1) * BS, p * W:(p + 1) * W] = value

        stage1(j, ring, 2, store)
        for first, n, left, right in (
            (5, 2, kphi[...], dn), (4, 1, kphi[:, :W], up), (7, 1, kphi_o[rows(j), :], qp), (1, 2, kphi[...], own),
        ):
            add(first, n, left, right[rows(j), :])
            for p in range(first, first + n):
                if done is not None:
                    done(p)

    inside = jnp.logical_and(s + core > 0, s + core < slabs).astype(F32)

    def beyond_face(p):
        return jnp.where(inside > 0, halo[p, 1], jnp.zeros((CH, W), BF16))

    def swap(p):
        return remote(acc.at[p, :, 1 - core], xr.at[p], c_s.at[p], c_r.at[p], across)

    def final(p, h):
        r, c = PAIRS[p]
        to = blk_at(((c[0] - r[0]) % 2, (c[1] - r[1]) % 4))
        piece = sb.at[p, h] if r == O else mid.at[p, h]
        cp = remote(piece, fr.at[mine], f_s.at[p, h], f_r.at[mine], (to * 4 + h * 2 + core, b))
        return cp, piece, jnp.logical_and(to == z, h == xl)

    def move(p):
        return remote(sb.at[p], mid.at[p], m_s.at[p], m_r.at[p], (s, blk_at(PAIRS[p][0])))

    def settle(p):
        for h in range(2):
            cp, piece, stays = final(p, h)

            @pl.when(stays)
            def _():
                fr[mine] = piece[...]

            @pl.when(jnp.logical_not(stays))
            def _():
                cp.start()

    def leave(p):
        swap(p).wait_recv()
        sb[p] = (acc[p, :, core] + xr[p]).astype(BF16)
        if PAIRS[p][0] == O:
            settle(p)
        else:
            move(p).start()

    lag = 2

    @pl.loop(0, nch + lag)
    def _(t):
        @pl.when(t < nch)
        def _():
            send_d(t).wait_recv()
            send_q(t).start()

        @pl.when(t + AHEAD < nch)
        def _():
            send_u(t + AHEAD).start()
            send_d(t + AHEAD).start()

        @pl.when(t + AHEAD == nch)
        def _():
            ho_out.wait_recv()
            hu_out.start()
            hx_out.wait_recv()
            hq_out.start()

        for k in range(5):
            @pl.when(t == 2 * k + 2)
            def _():
                if k > 0:
                    hear(k - 1)
                if k < 4:
                    tell(k)

        @pl.when(t == 0)
        def _():
            ho_in.wait_recv()
            fill(ring_o, 0, (halo[0, 0],))

        @pl.when(t < nch)
        def _():
            fill(ring_o, (t + 1) & 3, (own[rows(t), :],))

        @pl.when(t == nch)
        def _():
            fill(ring_o, (nch + 1) & 3, (beyond_face(0),))

        @pl.when(jnp.logical_and(t >= 1, t <= nch))
        def _():
            send_u(t - 1).wait_recv()
            early(t - 1)

        @pl.when(t == nch)
        def _():
            for p in EARLY:
                swap(p).start()

        j = t - lag

        @pl.when(j == 0)
        def _():
            hu_in.start()
            send_q(0).wait_recv()
            hq_in.start()
            hu_in.wait_recv()
            hq_in.wait_recv()
            fill(ring, 0, (halo[1, 0], halo[2, 0]))

        @pl.when(j >= 0)
        def _():
            @pl.when(j > 0)
            def _():
                send_q(j).wait_recv()

            fill(ring, (j + 1) & 3, (qp[rows(j), :], up[rows(j), :]))

        @pl.when(j >= 1)
        def _():
            late(j - 1)

    hu_out.wait_recv()
    hq_out.wait_recv()
    fill(ring, (nch + 1) & 3, (beyond_face(1), beyond_face(2)))
    for p in EARLY:
        leave(p)
    late(nch - 1, lambda p: swap(p).start())

    for p, arrived in STEPS:
        if arrived:
            move(p).wait_recv()
            settle(p)
        else:
            leave(p)

    out[...] = jnp.zeros((BS, W), F32)

    @pl.loop(0, 16)
    def _(i):
        @pl.when(i != mine)
        def _():
            remote(sb.at[0, 0], fr.at[i], f_s.at[0, 0], f_r.at[i], across).wait_recv()

        out[...] += fr[i].astype(F32)

    for cp in (ho_out, ho_in, hu_out, hu_in, hq_out, hq_in, hx_out):
        cp.wait_send()

    @pl.loop(0, nch)
    def _(t):
        send_u(t).wait_send()
        send_d(t).wait_send()
        send_q(t).wait_send()

    for p in range(8):
        swap(p).wait_send()
        if PAIRS[p][0] != O:
            move(p).wait_send()
        for h in range(2):
            cp, _, stays = final(p, h)

            @pl.when(jnp.logical_not(stays))
            def _():
                cp.wait_send()


def body(modes, stiffness, offsets):
    n, w = modes.shape
    nch = n // CH
    dma = pltpu.SemaphoreType.DMA
    res = pl.pallas_call(
        kernel,
        out_shape=jax.ShapeDtypeStruct((BS, W), F32),
        in_specs=[
            pl.BlockSpec(memory_space=pl.ANY),
            pl.BlockSpec(memory_space=pl.ANY),
            pl.BlockSpec(memory_space=pl.ANY),
        ],
        out_specs=pl.BlockSpec(memory_space=pltpu.VMEM),
        scratch_shapes=[
            pltpu.SMEM(offsets.shape[::-1], jnp.int32),
            pltpu.VMEM((n, w), BF16),
            pltpu.VMEM((n, 8 * BS), BF16),
            pltpu.VMEM((n, w), BF16),
            pltpu.VMEM((n, w), BF16),
            pltpu.VMEM((n, w), BF16),
            pltpu.VMEM((3, 2, CH, w), BF16),
            pltpu.VMEM((CH, w), BF16),
            pltpu.VMEM((4 * BPC, BS, W), BF16),
            pltpu.VMEM((4 * BPC, BS, 2 * W), BF16),
            pltpu.VMEM((n, W), BF16),
            pltpu.VMEM((CH, 2 * W), BF16),
            pltpu.VMEM((8, 2, 2, BS, W), F32),
            pltpu.VMEM((8, 2, BS, W), F32),
            pltpu.VMEM((8, 2, BS, W), BF16),
            pltpu.VMEM((8, 2, BS, W), BF16),
            pltpu.VMEM((16, BS, W), BF16),
            dma((3,)),
            dma((nch,)), dma((nch,)), dma((nch,)), dma((nch,)), dma((nch,)), dma((nch,)),
            dma((7,)), dma((7,)), dma((8,)), dma((8,)), dma((8, 2)), dma((16,)), dma((8,)), dma((8,)),
            pltpu.SemaphoreType.REGULAR((7,)),
        ],
        compiler_params=pltpu.CompilerParams(
            collective_id=0, has_side_effects=True, vmem_limit_bytes=60 * 2**20
        ),
    )(modes, stiffness, offsets.T)
    return res.T


def solution(mesh):
    in_specs = (P("slab", "blk"), P("slab", None), P("slab", None))
    return jax.shard_map(body, mesh=mesh, in_specs=in_specs, out_specs=P("blk", "slab"), check_vma=False)
```

```python
import jax
import jax.numpy as jnp
from jax import lax
from jax.experimental import pallas as pl
from jax.experimental.pallas import tpu as pltpu
from jax.sharding import PartitionSpec as P

MESH = pl.DeviceIdType.MESH
BS = 64
CH = 256
BPC = CH // BS
W = 256
F32 = jnp.float32
BF16 = jnp.bfloat16

O, U, D, Q = (0, 0), (0, 1), (0, 3), (1, 3)
PAIRS = ((O, O), (O, Q), (O, U), (U, O), (U, Q), (D, Q), (D, U), (Q, O))
EARLY = (3, 0)
STEPS = (
    (5, False), (4, False), (6, False), (7, False), (1, False), (2, False),
    (3, True), (5, True), (4, True), (6, True), (7, True),
)
AHEAD = 3


def kernel(
    modes, stiff, offsets, out,
    offs, own, kv, up, dn, qp, halo, hmid, ring_o, ring, kphi_o, kphi, acc, xr, sb, mid, fr,
    lsem, yu_s, yu_r, yd_s, yd_r, xq_s, xq_r, h_s, h_r, c_s, c_r, f_s, f_r, m_s, m_r, tok,
):
    s, b = lax.axis_index("slab"), lax.axis_index("blk")
    z, xl, core = s // 4, (s // 2) % 2, s % 2
    xh, y = b // 4, b % 4
    nch = modes.shape[0] // CH
    slabs = lax.axis_size("slab")

    def blk_at(d):
        return ((xh + d[0]) % 2) * 4 + (y + d[1]) % 4

    outer = lax.rem(s + 2 * core - 1 + slabs, slabs)
    inner = s + 1 - 2 * core
    y_up, y_dn, x_far = (s, blk_at((0, 1))), (s, blk_at((0, 3))), (s, blk_at((1, 0)))
    across, beyond = (inner, b), (outer, b)

    def chunk(t):
        return t * core + (nch - 1 - t) * (1 - core)

    def rows(t):
        return pl.ds(pl.multiple_of(chunk(t) * CH, CH), CH)

    way = 2 * core - 1

    aside = (outer, blk_at((1, 0)))

    z_up, z_dn = (lax.rem(s + 4, slabs), b), (lax.rem(s + slabs - 4, slabs), b)
    beside = (s + 2 - 4 * xl, b)
    mine = z * 2 + xl

    copy_k = pltpu.make_async_copy(stiff, kv, lsem.at[0])
    copy_o = pltpu.make_async_copy(modes, own, lsem.at[1])
    copy_f = pltpu.make_async_copy(offsets, offs, lsem.at[2])
    copy_f.start()
    copy_k.start()
    copy_o.start()

    barrier = pltpu.get_barrier_semaphore()
    near = (y_up, y_dn, x_far, across, beyond, aside, (s, blk_at((1, 1))), z_up, z_dn, beside)
    for dev in near:
        pl.semaphore_signal(barrier, inc=1, device_id=dev, device_id_type=MESH)
    pl.semaphore_wait(barrier, len(near))

    def tell(k):
        if k < 3:
            pl.semaphore_signal(tok.at[2 * k], inc=1, device_id=z_up, device_id_type=MESH)
            pl.semaphore_signal(tok.at[2 * k + 1], inc=1, device_id=z_dn, device_id_type=MESH)
        else:
            pl.semaphore_signal(tok.at[6], inc=1, device_id=beside, device_id_type=MESH)

    def hear(k):
        if k < 3:
            pl.semaphore_wait(tok.at[2 * k], 1)
            pl.semaphore_wait(tok.at[2 * k + 1], 1)
        else:
            pl.semaphore_wait(tok.at[6], 1)

    def remote(src, dst, ssem, rsem, dev):
        return pltpu.make_async_remote_copy(src, dst, ssem, rsem, device_id=dev, device_id_type=MESH)

    def send_u(t):
        return remote(modes.at[rows(t)], up.at[rows(t)], yu_s.at[t], yu_r.at[t], y_dn)

    def send_d(t):
        return remote(modes.at[rows(t)], dn.at[rows(t)], yd_s.at[t], yd_r.at[t], y_up)

    def send_q(t):
        return remote(dn.at[rows(t)], qp.at[rows(t)], xq_s.at[t], xq_r.at[t], x_far)

    ho_out = remote(modes.at[rows(nch - 1)], halo.at[0, 1], h_s.at[0], h_r.at[0], beyond)
    ho_in = remote(modes.at[rows(0)], halo.at[0, 0], h_s.at[1], h_r.at[1], across)
    hu_out = remote(halo.at[0, 1], halo.at[2, 1], h_s.at[2], h_r.at[2], y_dn)
    hu_in = remote(up.at[rows(0)], halo.at[2, 0], h_s.at[3], h_r.at[3], across)
    hq_out = remote(hmid, halo.at[1, 1], h_s.at[4], h_r.at[4], y_up)
    hq_in = remote(qp.at[rows(0)], halo.at[1, 0], h_s.at[5], h_r.at[5], across)

    hx_out = remote(modes.at[rows(nch - 1)], hmid, h_s.at[6], h_r.at[6], aside)

    ho_out.start()
    hx_out.start()
    ho_in.start()

    @pl.loop(0, AHEAD)
    def _(t):
        send_u(t).start()
        send_d(t).start()

    acc[...] = jnp.zeros_like(acc)
    copy_f.wait()
    copy_k.wait()
    copy_o.wait()

    def fill(ref, slot, parts):
        for p, part in enumerate(parts):
            ref[pl.ds(slot * BPC, BPC), :, p * W:(p + 1) * W] = part.reshape(BPC, BS, W)

    def stage1(j, ref, panels, store):
        c = chunk(j)
        for i in range(BPC):
            line = c * BPC + i
            where = []
            for col in range(8):
                pos = offs[col, line] + i
                slot = (j + 1 + way * (pos >> 2)) & 3
                where.append(slot * BPC + (pos & 3))
            lhs = kv[pl.ds(pl.multiple_of(line * BS, BS), BS), :]
            for p in range(panels):
                gathered = jnp.concatenate([ref[w, :, p * W:(p + 1) * W] for w in where], axis=0)
                store(i, p, jnp.dot(lhs, gathered, preferred_element_type=F32).astype(BF16))

    def add(first, n, left, right):
        prod = lax.dot_general(left, right, (((0,), (0,)), ((), ())), preferred_element_type=F32)
        acc[first:first + n] += prod.reshape(n, 2, 2, BS, W)

    def early(j):
        base = chunk(j) * CH

        def store(i, p, value):
            kphi_o[pl.ds(pl.multiple_of(base + i * BS, BS), BS), :] = value

        stage1(j, ring_o, 1, store)
        for ref, p in ((up, 3), (own, 0)):
            add(p, 1, kphi_o[rows(j), :], ref[rows(j), :])

    def late(j, done=None):
        def store(i, p, value):
            kphi[i * BS:(i + 1) * BS, p * W:(p + 1) * W] = value

        stage1(j, ring, 2, store)
        for first, n, left, right in (
            (5, 2, kphi[...], dn), (4, 1, kphi[:, :W], up), (7, 1, kphi_o[rows(j), :], qp), (1, 2, kphi[...], own),
        ):
            add(first, n, left, right[rows(j), :])
            for p in range(first, first + n):
                if done is not None:
                    done(p)

    inside = jnp.logical_and(s + core > 0, s + core < slabs).astype(F32)

    def beyond_face(p):
        return jnp.where(inside > 0, halo[p, 1], jnp.zeros((CH, W), BF16))

    def swap(p):
        return remote(acc.at[p, :, 1 - core], xr.at[p], c_s.at[p], c_r.at[p], across)

    def final(p, h):
        r, c = PAIRS[p]
        to = blk_at(((c[0] - r[0]) % 2, (c[1] - r[1]) % 4))
        piece = sb.at[p, h] if r == O else mid.at[p, h]
        cp = remote(piece, fr.at[mine], f_s.at[p, h], f_r.at[mine], (to * 4 + h * 2 + core, b))
        return cp, piece, jnp.logical_and(to == z, h == xl)

    def move(p):
        return remote(sb.at[p], mid.at[p], m_s.at[p], m_r.at[p], (s, blk_at(PAIRS[p][0])))

    def settle(p):
        for h in range(2):
            cp, piece, stays = final(p, h)

            @pl.when(stays)
            def _():
                fr[mine] = piece[...]

            @pl.when(jnp.logical_not(stays))
            def _():
                cp.start()

    def leave(p):
        swap(p).wait_recv()
        sb[p] = (acc[p, :, core] + xr[p]).astype(BF16)
        if PAIRS[p][0] == O:
            settle(p)
        else:
            move(p).start()

    lag = 2

    @pl.loop(0, nch + lag)
    def _(t):
        @pl.when(t < nch)
        def _():
            send_d(t).wait_recv()
            send_q(t).start()

        @pl.when(t + AHEAD < nch)
        def _():
            send_u(t + AHEAD).start()
            send_d(t + AHEAD).start()

        @pl.when(t + AHEAD == nch)
        def _():
            ho_out.wait_recv()
            hu_out.start()
            hx_out.wait_recv()
            hq_out.start()

        for k in range(5):
            @pl.when(t == 2 * k + 2)
            def _():
                if k > 0:
                    hear(k - 1)
                if k < 4:
                    tell(k)

        @pl.when(t == 0)
        def _():
            ho_in.wait_recv()
            fill(ring_o, 0, (halo[0, 0],))

        @pl.when(t < nch)
        def _():
            fill(ring_o, (t + 1) & 3, (own[rows(t), :],))

        @pl.when(t == nch)
        def _():
            fill(ring_o, (nch + 1) & 3, (beyond_face(0),))

        @pl.when(jnp.logical_and(t >= 1, t <= nch))
        def _():
            send_u(t - 1).wait_recv()
            early(t - 1)

        @pl.when(t == nch)
        def _():
            for p in EARLY:
                swap(p).start()

        j = t - lag

        @pl.when(j == 0)
        def _():
            hu_in.start()
            send_q(0).wait_recv()
            hq_in.start()
            hu_in.wait_recv()
            hq_in.wait_recv()
            fill(ring, 0, (halo[1, 0], halo[2, 0]))

        @pl.when(j >= 0)
        def _():
            @pl.when(j > 0)
            def _():
                send_q(j).wait_recv()

            fill(ring, (j + 1) & 3, (qp[rows(j), :], up[rows(j), :]))

        @pl.when(j >= 1)
        def _():
            late(j - 1)

    hu_out.wait_recv()
    hq_out.wait_recv()
    fill(ring, (nch + 1) & 3, (beyond_face(1), beyond_face(2)))
    for p in EARLY:
        leave(p)
    late(nch - 1, lambda p: swap(p).start())

    for p, arrived in STEPS:
        if arrived:
            move(p).wait_recv()
            settle(p)
        else:
            leave(p)

    out[...] = jnp.zeros((BS, W), F32)

    @pl.loop(0, 16)
    def _(i):
        @pl.when(i != mine)
        def _():
            remote(sb.at[0, 0], fr.at[i], f_s.at[0, 0], f_r.at[i], across).wait_recv()

        out[...] += fr[i].astype(F32)

    for cp in (ho_out, ho_in, hu_out, hu_in, hq_out, hq_in, hx_out):
        cp.wait_send()

    @pl.loop(0, nch)
    def _(t):
        send_u(t).wait_send()
        send_d(t).wait_send()
        send_q(t).wait_send()

    for p in range(8):
        swap(p).wait_send()
        if PAIRS[p][0] != O:
            move(p).wait_send()
        for h in range(2):
            cp, _, stays = final(p, h)

            @pl.when(jnp.logical_not(stays))
            def _():
                cp.wait_send()


def body(modes, stiffness, offsets):
    n, w = modes.shape
    nch = n // CH
    dma = pltpu.SemaphoreType.DMA
    res = pl.pallas_call(
        kernel,
        out_shape=jax.ShapeDtypeStruct((BS, W), F32),
        in_specs=[
            pl.BlockSpec(memory_space=pl.ANY),
            pl.BlockSpec(memory_space=pl.ANY),
            pl.BlockSpec(memory_space=pl.ANY),
        ],
        out_specs=pl.BlockSpec(memory_space=pltpu.VMEM),
        scratch_shapes=[
            pltpu.SMEM(offsets.shape[::-1], jnp.int32),
            pltpu.VMEM((n, w), BF16),
            pltpu.VMEM((n, 8 * BS), BF16),
            pltpu.VMEM((n, w), BF16),
            pltpu.VMEM((n, w), BF16),
            pltpu.VMEM((n, w), BF16),
            pltpu.VMEM((3, 2, CH, w), BF16),
            pltpu.VMEM((CH, w), BF16),
            pltpu.VMEM((4 * BPC, BS, W), BF16),
            pltpu.VMEM((4 * BPC, BS, 2 * W), BF16),
            pltpu.VMEM((n, W), BF16),
            pltpu.VMEM((CH, 2 * W), BF16),
            pltpu.VMEM((8, 2, 2, BS, W), F32),
            pltpu.VMEM((8, 2, BS, W), F32),
            pltpu.VMEM((8, 2, BS, W), BF16),
            pltpu.VMEM((8, 2, BS, W), BF16),
            pltpu.VMEM((16, BS, W), BF16),
            dma((3,)),
            dma((nch,)), dma((nch,)), dma((nch,)), dma((nch,)), dma((nch,)), dma((nch,)),
            dma((7,)), dma((7,)), dma((8,)), dma((8,)), dma((8, 2)), dma((16,)), dma((8,)), dma((8,)),
            pltpu.SemaphoreType.REGULAR((7,)),
        ],
        compiler_params=pltpu.CompilerParams(
            collective_id=0, has_side_effects=True, vmem_limit_bytes=60 * 2**20
        ),
    )(modes, stiffness, offsets.T)
    return res.T


def solution(mesh):
    in_specs = (P("slab", "blk"), P("slab", None), P("slab", None))
    return jax.shard_map(body, mesh=mesh, in_specs=in_specs, out_specs=P("blk", "slab"), check_vma=False)
```
